32 devices in a mesh: dp: 8 (over z, x), ctx: 4 (over y, core).
Axes of the slice: x: 2, y: 2, z: 4, core: 2. Of those that a mesh axis runs over, the one named last changes fastest.
Arguments:
- tokens: bfloat16 [32, 2560, 1280], P('dp', 'ctx'), may hold values from -64 to 64
- router: bfloat16 [1280, 64], replicated, may hold values from -1 to 1
- expert_up: bfloat16 [32, 1280, 2560], P(('dp', 'ctx')), may hold values from -0.5 to 0.5
- expert_down: bfloat16 [32, 2560, 1280], P(('dp', 'ctx')), may hold values from -0.25 to 0.25
Outputs:
- mixed: bfloat16 [32, 2560, 1280], P('dp', 'ctx')
The draws below stay inside these ranges and needn't reach their ends.
All inputs are finite; a program needn't handle non-finite values.
Results may differ from the reference program's by a relative error of at most 0.015.
Values may be sent and summed in bfloat16 or wider, within the bound.
A program may use at most 128 MiB of HBM per device.

```python
import math
import jax
import jax.numpy as jnp
from jax import lax

D = 1280
FF = 2560
PER_EXPERT = 2
TOK_DEV = 640
EXPERTS = 32
SLOTS = 64
CLIPS = 32
TOK = 2560
N_CTX = 4


def router_table(key):
    normal_draw = jax.random.normal(jax.random.fold_in(key, 7), (D, SLOTS), jnp.float32)
    lengths = jnp.sqrt(jnp.sum(normal_draw * normal_draw, axis=0))
    target = jnp.exp(jax.random.uniform(jax.random.fold_in(key, 8), (SLOTS,), jnp.float32, math.log(2.2), math.log(3.2)))
    return jnp.clip(normal_draw / lengths[None, :] * target[None, :], -1.0, 1.0)


def draw_router(key, part):
    return router_table(key).astype(jnp.bfloat16)


def draw_tokens(key, part):
    values = jnp.clip(jax.random.normal(jax.random.fold_in(key, 1), (CLIPS, TOK, D), jnp.float32), -6.0, 6.0)
    return values.astype(jnp.bfloat16)


def block_levels(key, dims, pieces, smallest, largest):
    def one(dim, blocks):
        steps = jax.random.uniform(jax.random.fold_in(jax.random.fold_in(key, 6), dim), (blocks,), jnp.float32, smallest / len(pieces), largest / len(pieces))
        return jnp.repeat(jnp.exp(steps), dims[dim] // blocks).reshape((-1,) + (1,) * (len(dims) - dim - 1))

    factor_of = one(*pieces[0])
    for cut in pieces[1:]:
        factor_of = factor_of * one(*cut)
    return factor_of


def noise(rng, shape, spread, bound, split=(), dtype=jnp.bfloat16):
    values = spread * jax.random.normal(rng, shape, jnp.float32)
    if split:
        values = values * block_levels(rng, shape, split, -0.22, 0.18)
    return jnp.clip(values, -bound, bound).astype(dtype)


def setup_inputs(seed: int = 0) -> dict:
    keys = jax.random.split(jax.random.key(seed), 5)
    tokens = draw_tokens(jax.random.fold_in(keys[4], 71), 0)
    router = draw_router(jax.random.fold_in(keys[4], 71), 0)
    expert_up = noise(keys[2], (EXPERTS, D, FF), (D // 9) ** -0.5, 0.5, ((0, 32),))
    expert_down = noise(keys[3], (EXPERTS, FF, D), (FF // 4) ** -0.5, 0.25, ((0, 32),))
    return {"tokens": tokens, "router": router, "expert_up": expert_up, "expert_down": expert_down}


def reference(tokens, router, expert_up, expert_down):
    def per_clip(clip_rows):
        logits = jnp.dot(clip_rows, router, preferred_element_type=jnp.float32)
        column_max = jnp.max(logits, axis=0)
        exponent = jnp.exp(logits - column_max[None, :])
        dispatch = (exponent / jnp.sum(exponent, axis=0)[None, :]).astype(jnp.bfloat16)
        blocks = jnp.einsum("btj,btd->bjd", dispatch.reshape(N_CTX, TOK_DEV, SLOTS).astype(jnp.float32), clip_rows.reshape(N_CTX, TOK_DEV, D).astype(jnp.float32))
        blocks = lax.optimization_barrier(blocks.astype(jnp.bfloat16)).astype(jnp.float32)
        slot_inputs = jnp.sum(blocks, axis=0).astype(jnp.bfloat16)
        row_max = jnp.max(logits, axis=1)
        row_exp = jnp.exp(logits - row_max[:, None])
        combine = (row_exp / jnp.sum(row_exp, axis=1)[:, None]).astype(jnp.bfloat16)
        return slot_inputs, combine

    slot_inputs, combine = lax.map(per_clip, tokens)
    grouped = jnp.moveaxis(slot_inputs.reshape(CLIPS, EXPERTS, PER_EXPERT, D), 1, 0)

    def per_expert(bundle):
        slot_rows, up_matrix, down_matrix = bundle
        flat = slot_rows.reshape(CLIPS * PER_EXPERT, D)
        hidden = jax.nn.gelu(jnp.dot(flat, up_matrix, preferred_element_type=jnp.float32), approximate=False).astype(jnp.bfloat16)
        produced = jnp.dot(hidden, down_matrix, preferred_element_type=jnp.float32).astype(jnp.bfloat16)
        return produced.reshape(CLIPS, PER_EXPERT, D)

    produced = lax.map(per_expert, (grouped, expert_up, expert_down))
    slot_outputs = jnp.moveaxis(produced, 0, 1).reshape(CLIPS, SLOTS, D)

    def per_mix(bundle):
        return jnp.dot(bundle[0], bundle[1], preferred_element_type=jnp.float32).astype(jnp.bfloat16)

    return lax.map(per_mix, (combine, slot_outputs))
```

```python
import functools

import jax
import jax.numpy as jnp
import numpy as np
from jax import lax
from jax.experimental import pallas as pl
from jax.experimental.pallas import tpu as pltpu
from jax.sharding import PartitionSpec as P

MESH = pl.DeviceIdType.MESH
CORES = 2
F32 = jnp.float32
BF16 = jnp.bfloat16
MIB = 2**20


def clip_rows(shape, clip, per_clip, group, dim=0):
    place = lax.rem(lax.broadcasted_iota(jnp.int32, shape, dim), group)
    return (place >= clip * per_clip) & (place < (clip + 1) * per_clip)


def exchange(
    dims, tok_hbm, router_hbm, spread_hbm, up_hbm, down_hbm, gathered_ref, combine_ref,
    tok, router, spread, routed, up, down, flipped, logit, diag, acc, hidden, part, from_core, chip, from_y, slab,
    rows_in, result, pool, stat, stats_in, columns,
    tok_sem, weight_sem, stat_sem, core_sem, y_sem, out_sem, back_sem, ysend_sem, fwd_sem,
):
    n_dp, n_ctx, clips, tok_dev, per_expert, chunks, width, staged = dims
    n_y = n_ctx // CORES
    group = clips * per_expert
    rows = n_dp * n_ctx * group
    dp = lax.axis_index("dp")
    ctx = lax.axis_index("ctx")
    y = ctx // CORES
    core = ctx % CORES
    other = 1 - core
    partner = (dp, y * CORES + other)
    far = [(kd, ky) for kd in range(n_dp) for ky in range(n_y) if (kd, ky) != (0, 0)]

    def place(kd, ky):
        return (lax.rem(dp + kd, n_dp), lax.rem(y + ky, n_y) * CORES + core)

    def lanes(f):
        return pl.ds(pl.multiple_of(f * width, width), width)

    def remote(src, dst, sems, index, target):
        return pltpu.make_async_remote_copy(
            src_ref=src, dst_ref=dst, send_sem=sems.at[(0,) + index], recv_sem=sems.at[(1,) + index],
            device_id=target, device_id_type=MESH,
        )

    def token_copy(c):
        there = tok.at[pl.ds(pl.multiple_of(c * tok_dev, tok_dev), tok_dev)]
        return pltpu.make_async_copy(tok_hbm.at[c], there, tok_sem.at[c])

    def stat_copy(k):
        return remote(stat, stats_in.at[k - 1], stat_sem, (k - 1,), (dp, lax.rem(ctx + k, n_ctx)))

    def core_copy(f):
        return remote(part.at[f, other], from_core.at[f], core_sem, (f,), partner)

    def y_copy(f, ky):
        target = place(0, ky)
        src = chip.at[f, lax.rem(y + ky, n_y)]
        return remote(src, from_y.at[f, ky - 1], y_sem, (f, ky - 1), target)

    def slab_copy(f, kd):
        target = place(kd, 0)
        return remote(slab.at[f, target[0]], rows_in.at[f, 0, dp], out_sem, (f, kd - 1), target)

    def direct_copy(f, i):
        target = place(*far[i])
        src = chip.at[f, lax.rem(y + far[i][1], n_y), target[0]]
        return remote(src, rows_in.at[f, y, dp], out_sem, (f, i), target)

    def back_copy(f, kd):
        target = place(kd, 0)
        return remote(result.at[f, target[0]], pool.at[f, core, y, dp], back_sem, (f, kd - 1), target)

    def back_direct(f, i):
        target = place(*far[i])
        return remote(result.at[f, target[0]], pool.at[f, core, y, dp], back_sem, (f, i), target)

    def spread_copy_y(f, ky):
        return remote(pool.at[f, core, y], pool.at[f, core, y], ysend_sem, (f, ky - 1), place(0, ky))

    def forward_copy(f):
        return remote(pool.at[f, core], pool.at[f, core], fwd_sem, (f,), partner)

    router_copy = pltpu.make_async_copy(router_hbm, router, weight_sem.at[2])
    router_copy.start()
    spread_copy = pltpu.make_async_copy(spread_hbm, spread, weight_sem.at[3])
    spread_copy.start()
    for c in range(clips):
        token_copy(c).start()
    up_copy = pltpu.make_async_copy(up_hbm.at[0], up, weight_sem.at[0])
    down_copy = pltpu.make_async_copy(down_hbm.at[0], down, weight_sem.at[1])

    def signal(target):
        pl.semaphore_signal(barrier, inc=1, device_id=target, device_id_type=MESH)

    barrier = pltpu.get_barrier_semaphore()
    for kd, ky in far:
        signal(place(kd, ky))
    for ky in range(n_y):
        signal((dp, lax.rem(y + ky, n_y) * CORES + other))

    router_copy.wait()
    spread_copy.wait()
    routed[...] = jnp.dot(spread[...], router[...], preferred_element_type=F32).T.astype(BF16)

    @pl.loop(0, clips)
    def _(c):
        token_copy(c).wait()
        rows_of = pl.ds(pl.multiple_of(c * tok_dev, tok_dev), tok_dev)
        here = jnp.dot(tok[rows_of, :], routed[...], preferred_element_type=F32)
        flipped[...] = jnp.where(clip_rows((tok_dev, rows), c, per_expert, group, 1), here, flipped[...])

    up_copy.start()
    down_copy.start()
    logit[...] = flipped[...].T
    highest = jnp.max(logit[...], axis=1, keepdims=True)
    powers = jnp.exp(logit[...] - highest)
    total = jnp.sum(powers, axis=1, keepdims=True)
    lane = lax.broadcasted_iota(jnp.int32, (rows, 128), 1)
    stat[...] = jnp.where(lane == 0, highest, total).T[0:8, :]
    pl.semaphore_wait(barrier, len(far) + n_y)
    for k in range(1, n_ctx):
        stat_copy(k).start()
    powers = powers.astype(BF16)
    for c in range(clips):
        keep = jnp.where(clip_rows((rows, 128), c, per_expert, group), 1.0, 0.0).astype(BF16)
        for t in range(0, tok_dev, 128):
            diag[:, pl.ds(c * tok_dev + t, 128)] = powers[:, t : t + 128] * keep

    @pl.loop(0, chunks)
    def _(f):
        value = jnp.dot(diag[...], tok[:, lanes(f)], preferred_element_type=F32)
        part[f] = value.reshape(CORES, n_y * n_dp, group, width).astype(BF16)
        core_copy(f).start()

    for k in range(1, n_ctx):
        stat_copy(k).wait_recv()
    best = [stat[0:1, :]] + [stats_in[k, 0:1, :] for k in range(n_ctx - 1)]
    amount = [stat[1:2, :]] + [stats_in[k, 1:2, :] for k in range(n_ctx - 1)]
    top = functools.reduce(jnp.maximum, best)
    shrink = [jnp.exp(b - top) for b in best]
    whole = functools.reduce(jnp.add, [a * s for a, s in zip(amount, shrink)])
    theirs = jnp.where(core == 0, shrink[n_ctx - 1], shrink[1])
    sub = lax.broadcasted_iota(jnp.int32, (128, rows), 0)
    scales = jnp.where(sub == 0, shrink[0] / whole, theirs / whole).T
    columns[...] = scales.reshape(CORES, n_y * n_dp, group, 128)

    def merge(f):
        core_copy(f).wait_recv()
        scales = columns[core]
        mine, theirs = scales[:, :, 0:1], scales[:, :, 1:2]
        value = part[f, core].astype(F32) * mine + from_core[f].astype(F32) * theirs
        chip[f] = value.astype(BF16).reshape(n_y, n_dp, group, width)

    @pl.loop(0, staged)
    def _(f):
        merge(f)
        for ky in range(1, n_y):
            y_copy(f, ky).start()

    @pl.loop(staged, chunks)
    def _(f):
        merge(f)
        rows_in[f, y, dp] = chip[f, y, dp]
        for i in range(len(far)):
            direct_copy(f, i).start()

    @pl.loop(0, staged)
    def _(f):
        value = chip[f, y].astype(F32)
        for ky in range(1, n_y):
            y_copy(f, ky).wait_recv()
            value = value + from_y[f, ky - 1].astype(F32)
        slab[f] = value.astype(BF16)
        rows_in[f, 0, dp] = slab[f, dp]
        for kd in range(1, n_dp):
            slab_copy(f, kd).start()

    blocks = logit[...].reshape(rows // group, group, tok_dev)
    peak = jnp.max(blocks, axis=0)

    def over_slots(values, reduce, neutral):
        out = values
        for c in range(clips):
            keep = clip_rows((group, tok_dev), c, per_expert, group)
            out = jnp.where(keep, reduce(jnp.where(keep, values, neutral), axis=0, keepdims=True), out)
        return out

    peak = over_slots(peak, jnp.max, -jnp.inf)
    powers = jnp.exp(blocks - peak[None])
    norm = over_slots(jnp.sum(powers, axis=0), jnp.sum, 0.0)
    combine_ref[...] = (powers / norm[None]).reshape(rows, tok_dev).T.astype(BF16)

    acc[...] = jnp.zeros_like(acc)
    up_copy.wait()

    def expand(f, value):
        value = value.reshape(n_dp * group, width).astype(BF16)
        row0 = pl.multiple_of(f * width, width)
        acc[...] += jnp.dot(value, up[pl.ds(row0, width), :], preferred_element_type=F32)

    @pl.loop(staged, chunks)
    def _(f):
        for i in range(len(far)):
            direct_copy(f, i).wait_recv()
        value = rows_in[f, 0].astype(F32)
        for k in range(1, n_y):
            value = value + rows_in[f, k].astype(F32)
        expand(f, value)

    @pl.loop(0, staged)
    def _(f):
        for kd in range(1, n_dp):
            slab_copy(f, kd).wait_recv()
        expand(f, rows_in[f, 0].astype(F32))

    value = acc[...]
    hidden[...] = (0.5 * value * (1.0 + lax.erf(value * np.float32(np.sqrt(0.5))))).astype(BF16)
    down_copy.wait()

    def contract(f):
        value = jnp.dot(hidden[...], down[:, lanes(f)], preferred_element_type=F32)
        result[f] = value.reshape(n_dp, group, width).astype(BF16)
        pool[f, core, y, dp] = result[f, dp]

    @pl.loop(0, staged)
    def _(f):
        contract(f)
        for kd in range(1, n_dp):
            back_copy(f, kd).start()

    @pl.loop(staged, chunks)
    def _(f):
        contract(f)
        for i in range(len(far)):
            back_direct(f, i).start()

    @pl.loop(0, staged)
    def _(f):
        for kd in range(1, n_dp):
            back_copy(f, kd).wait_recv()
        for ky in range(1, n_y):
            spread_copy_y(f, ky).start()

    @pl.loop(0, staged)
    def _(f):
        for ky in range(1, n_y):
            spread_copy_y(f, ky).wait_recv()
        forward_copy(f).start()

    @pl.loop(staged, chunks)
    def _(f):
        for i in range(len(far)):
            back_direct(f, i).wait_recv()
        forward_copy(f).start()

    @pl.loop(0, chunks)
    def _(f):
        forward_copy(f).wait_recv()
        gathered_ref[f] = pool[f].astype(F32).reshape(rows, width).astype(BF16)

    for k in range(1, n_ctx):
        stat_copy(k).wait_send()

    @pl.loop(0, chunks)
    def _(f):
        core_copy(f).wait_send()
        forward_copy(f).wait_send()

    @pl.loop(0, staged)
    def _(f):
        for ky in range(1, n_y):
            y_copy(f, ky).wait_send()
            spread_copy_y(f, ky).wait_send()
        for kd in range(1, n_dp):
            slab_copy(f, kd).wait_send()
            back_copy(f, kd).wait_send()

    @pl.loop(staged, chunks)
    def _(f):
        for i in range(len(far)):
            direct_copy(f, i).wait_send()
            back_direct(f, i).wait_send()


def mix(clips, per_expert, chunks, width, parts, combine_ref, gathered_ref, out_hbm, stage, sem):
    tok_dev = combine_ref.shape[0]
    group = clips * per_expert
    size = tok_dev // parts
    copies = []
    for c in range(clips):
        for p in range(parts):
            piece = combine_ref[pl.ds(p * size, size), :]
            keep = clip_rows(piece.shape, c, per_expert, group, 1)
            weights = jnp.where(keep, piece.astype(F32), 0.0).astype(BF16)
            here = pl.ds(p * size, size)
            for f in range(chunks):
                stage[c, here, pl.ds(f * width, width)] = jnp.dot(
                    weights, gathered_ref[f], preferred_element_type=F32
                ).astype(BF16)
            copy = pltpu.make_async_copy(stage.at[c, here], out_hbm.at[c, here], sem.at[c, p])
            copy.start()
            copies.append(copy)
    for copy in copies:
        copy.wait()


def shards(n_dp, n_ctx, tokens, router, expert_up, expert_down):
    clips, tok_dev, feature = tokens.shape
    slots = router.shape[1]
    hidden = expert_up.shape[2]
    per_expert = slots // (n_dp * n_ctx)
    n_y = n_ctx // CORES
    group = clips * per_expert
    rows = n_dp * n_ctx * group
    width = 256
    parts = 2
    chunks = feature // width
    order = np.arange(slots).reshape(n_dp, n_y, CORES, 1, per_expert).transpose(2, 1, 0, 3, 4)
    order = np.broadcast_to(order, (CORES, n_y, n_dp, clips, per_expert)).reshape(-1)
    spread = jnp.asarray(order[:, None] == np.arange(slots)[None, :], BF16)
    staged = 2
    dims = (n_dp, n_ctx, clips, tok_dev, per_expert, chunks, width, staged)
    vmem = pl.BlockSpec(memory_space=pltpu.VMEM)
    hbm = pl.BlockSpec(memory_space=pl.ANY)
    piece = (n_dp, group, width)
    n_far = n_dp * n_y - 1
    dma = pltpu.SemaphoreType.DMA
    gathered, combine = pl.pallas_call(
        functools.partial(exchange, dims),
        out_shape=(
            pltpu.VMEM((chunks, rows, width), BF16),
            pltpu.VMEM((tok_dev, rows), BF16),
        ),
        in_specs=[hbm] * 5,
        out_specs=(vmem, vmem),
        scratch_shapes=[
            pltpu.VMEM((clips * tok_dev, feature), BF16),
            pltpu.VMEM((slots, feature), BF16),
            pltpu.VMEM((rows, slots), BF16),
            pltpu.VMEM((feature, rows), BF16),
            pltpu.VMEM((feature, hidden), BF16),
            pltpu.VMEM((hidden, feature), BF16),
            pltpu.VMEM((tok_dev, rows), F32),
            pltpu.VMEM((rows, tok_dev), F32),
            pltpu.VMEM((rows, clips * tok_dev), BF16),
            pltpu.VMEM((n_dp * group, hidden), F32),
            pltpu.VMEM((n_dp * group, hidden), BF16),
            pltpu.VMEM((chunks, CORES, n_y * n_dp, group, width), BF16),
            pltpu.VMEM((chunks, n_y * n_dp, group, width), BF16),
            pltpu.VMEM((chunks, n_y) + piece, BF16),
            pltpu.VMEM((chunks, n_y - 1) + piece, BF16),
            pltpu.VMEM((chunks,) + piece, BF16),
            pltpu.VMEM((chunks, n_y) + piece, BF16),
            pltpu.VMEM((chunks,) + piece, BF16),
            pltpu.VMEM((chunks, CORES, n_y) + piece, BF16),
            pltpu.VMEM((8, rows), F32),
            pltpu.VMEM((n_ctx - 1, 8, rows), F32),
            pltpu.VMEM((CORES, n_y * n_dp, group, 128), F32),
            dma((clips,)),
            dma((4,)),
            dma((2, n_ctx - 1)),
            dma((2, chunks)),
            dma((2, chunks, n_y - 1)),
            dma((2, chunks, n_far)),
            dma((2, chunks, n_far)),
            dma((2, chunks, n_y - 1)),
            dma((2, chunks)),
        ],
        compiler_params=pltpu.CompilerParams(collective_id=0, has_side_effects=True, vmem_limit_bytes=58 * MIB),
        name="exchange",
    )(tokens, router.T, spread, expert_up, expert_down)
    gathered = pltpu.with_memory_space_constraint(gathered, pltpu.VMEM)
    combine = pltpu.with_memory_space_constraint(combine, pltpu.VMEM)
    return pl.pallas_call(
        functools.partial(mix, clips, per_expert, chunks, width, parts),
        out_shape=jax.ShapeDtypeStruct(tokens.shape, BF16),
        in_specs=[vmem, vmem],
        out_specs=hbm,
        scratch_shapes=[pltpu.VMEM(tokens.shape, BF16), dma((clips, parts))],
        compiler_params=pltpu.CompilerParams(vmem_limit_bytes=32 * MIB),
        name="mix",
    )(combine, gathered)


def solution(mesh):
    in_specs = (
        P("dp", "ctx", None),
        P(),
        P(("dp", "ctx"), None, None),
        P(("dp", "ctx"), None, None),
    )
    out_specs = P("dp", "ctx", None)
    body = functools.partial(shards, mesh.shape["dp"], mesh.shape["ctx"])
    return jax.shard_map(body, mesh=mesh, in_specs=in_specs, out_specs=out_specs, check_vma=False)
```

```python
import functools

import jax
import jax.numpy as jnp
import numpy as np
from jax import lax
from jax.experimental import pallas as pl
from jax.experimental.pallas import tpu as pltpu
from jax.sharding import PartitionSpec as P

MESH = pl.DeviceIdType.MESH
CORES = 2
F32 = jnp.float32
BF16 = jnp.bfloat16
MIB = 2**20


def clip_rows(shape, clip, per_clip, group, dim=0):
    place = lax.rem(lax.broadcasted_iota(jnp.int32, shape, dim), group)
    return (place >= clip * per_clip) & (place < (clip + 1) * per_clip)


def exchange(
    dims, tok_hbm, router_hbm, spread_hbm, up_hbm, down_hbm, gathered_ref, combine_ref,
    tok, router, spread, routed, up, down, flipped, logit, diag, acc, hidden, part, from_core, chip, from_y, slab,
    rows_in, result, pool, stat, stats_in, columns,
    tok_sem, weight_sem, stat_sem, core_sem, y_sem, slab_sem, direct_sem, back_sem, back_direct_sem, ysend_sem, fwd_sem,
):
    n_dp, n_ctx, clips, tok_dev, per_expert, chunks, width, staged = dims
    n_y = n_ctx // CORES
    group = clips * per_expert
    rows = n_dp * n_ctx * group
    dp = lax.axis_index("dp")
    ctx = lax.axis_index("ctx")
    y = ctx // CORES
    core = ctx % CORES
    other = 1 - core
    partner = (dp, y * CORES + other)
    far = [(kd, ky) for kd in range(n_dp) for ky in range(n_y) if (kd, ky) != (0, 0)]

    def place(kd, ky):
        return (lax.rem(dp + kd, n_dp), lax.rem(y + ky, n_y) * CORES + core)

    def lanes(f):
        return pl.ds(pl.multiple_of(f * width, width), width)

    def remote(src, dst, sems, index, target):
        return pltpu.make_async_remote_copy(
            src_ref=src, dst_ref=dst, send_sem=sems.at[0], recv_sem=sems.at[1 + index],
            device_id=target, device_id_type=MESH,
        )

    def await_bytes(ref, sem):
        pltpu.make_async_copy(ref, ref, sem).wait()

    def token_copy(c):
        there = tok.at[pl.ds(pl.multiple_of(c * tok_dev, tok_dev), tok_dev)]
        return pltpu.make_async_copy(tok_hbm.at[c], there, tok_sem.at[c])

    def stat_copy(k):
        return remote(stat, stats_in.at[k - 1], stat_sem, 0, (dp, lax.rem(ctx + k, n_ctx)))

    def core_copy(f):
        return remote(part.at[f, other], from_core.at[f], core_sem, f, partner)

    def y_copy(f, ky):
        target = place(0, ky)
        src = chip.at[f, pl.ds(lax.rem(y + ky, n_y) * n_dp, n_dp)]
        return remote(src, from_y.at[f, ky - 1], y_sem, f, target)

    def slab_copy(f, kd):
        target = place(kd, 0)
        return remote(slab.at[f, target[0]], rows_in.at[f, dp], slab_sem, f, target)

    def direct_copy(f, i):
        target = place(*far[i])
        src = chip.at[f, lax.rem(y + far[i][1], n_y) * n_dp + target[0]]
        return remote(src, rows_in.at[f, y * n_dp + dp], direct_sem, f - staged, target)

    def back_copy(f, kd):
        target = place(kd, 0)
        return remote(result.at[f, target[0]], pool.at[f, core, y * n_dp + dp], back_sem, f, target)

    def back_direct(f, i):
        target = place(*far[i])
        return remote(result.at[f, target[0]], pool.at[f, core, y * n_dp + dp], back_direct_sem, f - staged, target)

    def ysend_copy(f, ky):
        piece = pool.at[f, core, pl.ds(y * n_dp, n_dp)]
        return remote(piece, piece, ysend_sem, f, place(0, ky))

    def forward_copy(f):
        return remote(pool.at[f, core], pool.at[f, core], fwd_sem, f, partner)

    n_far = len(far)
    straight = chunks - staged

    router_copy = pltpu.make_async_copy(router_hbm, router, weight_sem.at[2])
    router_copy.start()
    spread_copy = pltpu.make_async_copy(spread_hbm, spread, weight_sem.at[3])
    spread_copy.start()
    for c in range(clips):
        token_copy(c).start()
    up_copy = pltpu.make_async_copy(up_hbm.at[0], up, weight_sem.at[0])
    down_copy = pltpu.make_async_copy(down_hbm.at[0], down, weight_sem.at[1])

    def signal(target):
        pl.semaphore_signal(barrier, inc=1, device_id=target, device_id_type=MESH)

    barrier = pltpu.get_barrier_semaphore()
    for kd, ky in far:
        signal(place(kd, ky))
    for ky in range(n_y):
        signal((dp, lax.rem(y + ky, n_y) * CORES + other))

    router_copy.wait()
    spread_copy.wait()
    routed[...] = jnp.dot(spread[...], router[...], preferred_element_type=F32).T.astype(BF16)

    @pl.loop(0, clips)
    def _(c):
        token_copy(c).wait()
        rows_of = pl.ds(pl.multiple_of(c * tok_dev, tok_dev), tok_dev)
        here = jnp.dot(tok[rows_of, :], routed[...], preferred_element_type=F32)
        flipped[...] = jnp.where(clip_rows((tok_dev, rows), c, per_expert, group, 1), here, flipped[...])

    up_copy.start()
    down_copy.start()
    logit[...] = flipped[...].T
    highest = jnp.max(logit[...], axis=1, keepdims=True)
    powers = jnp.exp(logit[...] - highest)
    total = jnp.sum(powers, axis=1, keepdims=True)
    lane = lax.broadcasted_iota(jnp.int32, (rows, 128), 1)
    stat[...] = jnp.where(lane == 0, highest, total).T[0:8, :]
    pl.semaphore_wait(barrier, len(far) + n_y)
    for k in range(1, n_ctx):
        stat_copy(k).start()
    powers = powers.astype(BF16)
    for c in range(clips):
        keep = jnp.where(clip_rows((rows, 128), c, per_expert, group), 1.0, 0.0).astype(BF16)
        for t in range(0, tok_dev, 128):
            diag[:, pl.ds(c * tok_dev + t, 128)] = powers[:, t : t + 128] * keep

    @pl.loop(0, chunks)
    def _(f):
        value = jnp.dot(diag[...], tok[:, lanes(f)], preferred_element_type=F32)
        part[f] = value.reshape(CORES, n_y * n_dp, group, width).astype(BF16)
        core_copy(f).start()

    await_bytes(stats_in, stat_sem.at[1])
    best = [stat[0:1, :]] + [stats_in[k, 0:1, :] for k in range(n_ctx - 1)]
    amount = [stat[1:2, :]] + [stats_in[k, 1:2, :] for k in range(n_ctx - 1)]
    top = functools.reduce(jnp.maximum, best)
    shrink = [jnp.exp(b - top) for b in best]
    whole = functools.reduce(jnp.add, [a * s for a, s in zip(amount, shrink)])
    theirs = jnp.where(core == 0, shrink[n_ctx - 1], shrink[1])
    sub = lax.broadcasted_iota(jnp.int32, (128, rows), 0)
    scales = jnp.where(sub == 0, shrink[0] / whole, theirs / whole).T
    columns[...] = scales.reshape(CORES, n_y * n_dp, group, 128)

    def merge(f):
        core_copy(f).wait_recv()
        scales = columns[core]
        mine, theirs = scales[:, :, 0:1], scales[:, :, 1:2]
        value = part[f, core].astype(F32) * mine + from_core[f].astype(F32) * theirs
        chip[f] = value.astype(BF16)

    @pl.loop(0, staged)
    def _(f):
        merge(f)
        for ky in range(1, n_y):
            y_copy(f, ky).start()

    @pl.loop(staged, chunks)
    def _(f):
        merge(f)
        rows_in[f, y * n_dp + dp] = chip[f, y * n_dp + dp]
        for i in range(len(far)):
            direct_copy(f, i).start()

    @pl.loop(0, staged)
    def _(f):
        await_bytes(from_y.at[f], y_sem.at[1 + f])
        value = chip[f, pl.ds(y * n_dp, n_dp)].astype(F32)
        for ky in range(1, n_y):
            value = value + from_y[f, ky - 1].astype(F32)
        slab[f] = value.astype(BF16)
        rows_in[f, dp] = slab[f, dp]
        for kd in range(1, n_dp):
            slab_copy(f, kd).start()

    blocks = logit[...].reshape(rows // group, group, tok_dev)
    peak = jnp.max(blocks, axis=0)

    def over_slots(values, reduce, neutral):
        out = values
        for c in range(clips):
            keep = clip_rows((group, tok_dev), c, per_expert, group)
            out = jnp.where(keep, reduce(jnp.where(keep, values, neutral), axis=0, keepdims=True), out)
        return out

    peak = over_slots(peak, jnp.max, -jnp.inf)
    powers = jnp.exp(blocks - peak[None])
    norm = over_slots(jnp.sum(powers, axis=0), jnp.sum, 0.0)
    combine_ref[...] = (powers / norm[None]).reshape(rows, tok_dev).T.astype(BF16)

    acc[...] = jnp.zeros_like(acc)
    up_copy.wait()

    def expand(f, value):
        value = value.reshape(n_dp * group, width).astype(BF16)
        row0 = pl.multiple_of(f * width, width)
        acc[...] += jnp.dot(value, up[pl.ds(row0, width), :], preferred_element_type=F32)

    @pl.loop(staged, chunks)
    def _(f):
        await_bytes(rows_in.at[f, pl.ds(0, n_far)], direct_sem.at[1 + f - staged])
        value = rows_in[f, pl.ds(0, n_dp)].astype(F32)
        for k in range(1, n_y):
            value = value + rows_in[f, pl.ds(k * n_dp, n_dp)].astype(F32)
        expand(f, value)

    @pl.loop(0, staged)
    def _(f):
        await_bytes(rows_in.at[f, pl.ds(0, n_dp - 1)], slab_sem.at[1 + f])
        expand(f, rows_in[f, pl.ds(0, n_dp)].astype(F32))

    value = acc[...]
    hidden[...] = (0.5 * value * (1.0 + lax.erf(value * np.float32(np.sqrt(0.5))))).astype(BF16)
    down_copy.wait()

    def contract(f):
        value = jnp.dot(hidden[...], down[:, lanes(f)], preferred_element_type=F32)
        result[f] = value.reshape(n_dp, group, width).astype(BF16)
        pool[f, core, y * n_dp + dp] = result[f, dp]

    @pl.loop(0, staged)
    def _(f):
        contract(f)
        for kd in range(1, n_dp):
            back_copy(f, kd).start()

    @pl.loop(staged, chunks)
    def _(f):
        contract(f)
        for i in range(len(far)):
            back_direct(f, i).start()

    @pl.loop(0, staged)
    def _(f):
        await_bytes(result.at[f, pl.ds(0, n_dp - 1)], back_sem.at[1 + f])
        for ky in range(1, n_y):
            ysend_copy(f, ky).start()

    @pl.loop(0, staged)
    def _(f):
        await_bytes(from_y.at[f], ysend_sem.at[1 + f])
        forward_copy(f).start()

    @pl.loop(staged, chunks)
    def _(f):
        await_bytes(pool.at[f, core, pl.ds(0, n_far)], back_direct_sem.at[1 + f - staged])
        forward_copy(f).start()

    @pl.loop(0, chunks)
    def _(f):
        forward_copy(f).wait_recv()
        gathered_ref[f] = pool[f].astype(F32).reshape(rows, width).astype(BF16)

    await_bytes(stats_in, stat_sem.at[0])
    await_bytes(from_core, core_sem.at[0])
    await_bytes(pool.at[:, core], fwd_sem.at[0])
    if staged:
        await_bytes(from_y.at[pl.ds(0, staged)], y_sem.at[0])
        await_bytes(from_y.at[pl.ds(0, staged)], ysend_sem.at[0])
        await_bytes(slab.at[pl.ds(0, staged), pl.ds(0, n_dp - 1)], slab_sem.at[0])
        await_bytes(result.at[pl.ds(0, staged), pl.ds(0, n_dp - 1)], back_sem.at[0])
    if straight:
        await_bytes(chip.at[pl.ds(0, straight), pl.ds(0, n_far)], direct_sem.at[0])
        await_bytes(chip.at[pl.ds(0, straight), pl.ds(0, n_far)], back_direct_sem.at[0])


def mix(clips, per_expert, chunks, width, parts, combine_ref, gathered_ref, out_hbm, stage, sem):
    tok_dev = combine_ref.shape[0]
    group = clips * per_expert
    size = tok_dev // parts
    copies = []
    for c in range(clips):
        for p in range(parts):
            piece = combine_ref[pl.ds(p * size, size), :]
            keep = clip_rows(piece.shape, c, per_expert, group, 1)
            weights = jnp.where(keep, piece.astype(F32), 0.0).astype(BF16)
            here = pl.ds(p * size, size)
            for f in range(chunks):
                stage[c, here, pl.ds(f * width, width)] = jnp.dot(
                    weights, gathered_ref[f], preferred_element_type=F32
                ).astype(BF16)
            copy = pltpu.make_async_copy(stage.at[c, here], out_hbm.at[c, here], sem.at[c, p])
            copy.start()
            copies.append(copy)
    for copy in copies:
        copy.wait()


def shards(n_dp, n_ctx, tokens, router, expert_up, expert_down):
    clips, tok_dev, feature = tokens.shape
    slots = router.shape[1]
    hidden = expert_up.shape[2]
    per_expert = slots // (n_dp * n_ctx)
    n_y = n_ctx // CORES
    group = clips * per_expert
    rows = n_dp * n_ctx * group
    width = 256
    parts = 2
    chunks = feature // width
    order = np.arange(slots).reshape(n_dp, n_y, CORES, 1, per_expert).transpose(2, 1, 0, 3, 4)
    order = np.broadcast_to(order, (CORES, n_y, n_dp, clips, per_expert)).reshape(-1)
    spread = jnp.asarray(order[:, None] == np.arange(slots)[None, :], BF16)
    staged = 2
    dims = (n_dp, n_ctx, clips, tok_dev, per_expert, chunks, width, staged)
    vmem = pl.BlockSpec(memory_space=pltpu.VMEM)
    hbm = pl.BlockSpec(memory_space=pl.ANY)
    piece = (n_dp, group, width)
    dma = pltpu.SemaphoreType.DMA
    gathered, combine = pl.pallas_call(
        functools.partial(exchange, dims),
        out_shape=(
            pltpu.VMEM((chunks, rows, width), BF16),
            pltpu.VMEM((tok_dev, rows), BF16),
        ),
        in_specs=[hbm] * 5,
        out_specs=(vmem, vmem),
        scratch_shapes=[
            pltpu.VMEM((clips * tok_dev, feature), BF16),
            pltpu.VMEM((slots, feature), BF16),
            pltpu.VMEM((rows, slots), BF16),
            pltpu.VMEM((feature, rows), BF16),
            pltpu.VMEM((feature, hidden), BF16),
            pltpu.VMEM((hidden, feature), BF16),
            pltpu.VMEM((tok_dev, rows), F32),
            pltpu.VMEM((rows, tok_dev), F32),
            pltpu.VMEM((rows, clips * tok_dev), BF16),
            pltpu.VMEM((n_dp * group, hidden), F32),
            pltpu.VMEM((n_dp * group, hidden), BF16),
            pltpu.VMEM((chunks, CORES, n_y * n_dp, group, width), BF16),
            pltpu.VMEM((chunks, n_y * n_dp, group, width), BF16),
            pltpu.VMEM((chunks, n_y * n_dp, group, width), BF16),
            pltpu.VMEM((chunks, n_y - 1) + piece, BF16),
            pltpu.VMEM((chunks,) + piece, BF16),
            pltpu.VMEM((chunks, n_y * n_dp, group, width), BF16),
            pltpu.VMEM((chunks,) + piece, BF16),
            pltpu.VMEM((chunks, CORES, n_y * n_dp, group, width), BF16),
            pltpu.VMEM((8, rows), F32),
            pltpu.VMEM((n_ctx - 1, 8, rows), F32),
            pltpu.VMEM((CORES, n_y * n_dp, group, 128), F32),
            dma((clips,)),
            dma((4,)),
            dma((2,)),
            dma((1 + chunks,)),
            dma((1 + staged,)),
            dma((1 + staged,)),
            dma((1 + chunks - staged,)),
            dma((1 + staged,)),
            dma((1 + chunks - staged,)),
            dma((1 + staged,)),
            dma((1 + chunks,)),
        ],
        compiler_params=pltpu.CompilerParams(collective_id=0, has_side_effects=True, vmem_limit_bytes=58 * MIB),
        name="exchange",
    )(tokens, router.T, spread, expert_up, expert_down)
    gathered = pltpu.with_memory_space_constraint(gathered, pltpu.VMEM)
    combine = pltpu.with_memory_space_constraint(combine, pltpu.VMEM)
    return pl.pallas_call(
        functools.partial(mix, clips, per_expert, chunks, width, parts),
        out_shape=jax.ShapeDtypeStruct(tokens.shape, BF16),
        in_specs=[vmem, vmem],
        out_specs=hbm,
        scratch_shapes=[pltpu.VMEM(tokens.shape, BF16), dma((clips, parts))],
        compiler_params=pltpu.CompilerParams(vmem_limit_bytes=32 * MIB),
        name="mix",
    )(combine, gathered)


def solution(mesh):
    in_specs = (
        P("dp", "ctx", None),
        P(),
        P(("dp", "ctx"), None, None),
        P(("dp", "ctx"), None, None),
    )
    out_specs = P("dp", "ctx", None)
    body = functools.partial(shards, mesh.shape["dp"], mesh.shape["ctx"])
    return jax.shard_map(body, mesh=mesh, in_specs=in_specs, out_specs=out_specs, check_vma=False)
```

```python
import functools

import jax
import jax.numpy as jnp
import numpy as np
from jax import lax
from jax.experimental import pallas as pl
from jax.experimental.pallas import tpu as pltpu
from jax.sharding import PartitionSpec as P

MESH = pl.DeviceIdType.MESH
CORES = 2
F32 = jnp.float32
BF16 = jnp.bfloat16
MIB = 2**20


def clip_rows(shape, clip, per_clip, group, dim=0):
    place = lax.rem(lax.broadcasted_iota(jnp.int32, shape, dim), group)
    return (place >= clip * per_clip) & (place < (clip + 1) * per_clip)


def exchange(
    dims, tok_hbm, router_hbm, spread_hbm, up_hbm, down_hbm, gathered_ref, combine_ref,
    tok, router, spread, routed, up, down, flipped, logit, diag, acc, hidden, part, from_core, chip, from_y, slab,
    rows_in, result, pool, stat, stats_in, columns,
    tok_sem, weight_sem, stat_sem, core_sem, y_sem, slab_sem, direct_sem, back_sem, back_direct_sem, ysend_sem, fwd_sem,
):
    n_dp, n_ctx, clips, tok_dev, per_expert, chunks, width, staged, backed = dims
    n_y = n_ctx // CORES
    group = clips * per_expert
    rows = n_dp * n_ctx * group
    dp = lax.axis_index("dp")
    ctx = lax.axis_index("ctx")
    y = ctx // CORES
    core = ctx % CORES
    other = 1 - core
    partner = (dp, y * CORES + other)
    far = [(kd, ky) for kd in range(n_dp) for ky in range(n_y) if (kd, ky) != (0, 0)]

    def place(kd, ky):
        return (lax.rem(dp + kd, n_dp), lax.rem(y + ky, n_y) * CORES + core)

    def lanes(f):
        return pl.ds(pl.multiple_of(f * width, width), width)

    def remote(src, dst, sems, index, target):
        return pltpu.make_async_remote_copy(
            src_ref=src, dst_ref=dst, send_sem=sems.at[0], recv_sem=sems.at[1 + index],
            device_id=target, device_id_type=MESH,
        )

    def await_bytes(ref, sem):
        pltpu.make_async_copy(ref, ref, sem).wait()

    def token_copy(c):
        there = tok.at[pl.ds(pl.multiple_of(c * tok_dev, tok_dev), tok_dev)]
        return pltpu.make_async_copy(tok_hbm.at[c], there, tok_sem.at[c])

    def stat_copy(k):
        return remote(stat, stats_in.at[k - 1], stat_sem, 0, (dp, lax.rem(ctx + k, n_ctx)))

    def core_copy(f):
        return remote(part.at[f, other], from_core.at[f], core_sem, f, partner)

    def y_copy(f, ky):
        target = place(0, ky)
        src = chip.at[f, pl.ds(lax.rem(y + ky, n_y) * n_dp, n_dp)]
        return remote(src, from_y.at[f, ky - 1], y_sem, f, target)

    def slab_copy(f, kd):
        target = place(kd, 0)
        return remote(slab.at[f, target[0]], rows_in.at[f, dp], slab_sem, f, target)

    def direct_copy(f, i):
        target = place(*far[i])
        src = chip.at[f, lax.rem(y + far[i][1], n_y) * n_dp + target[0]]
        return remote(src, rows_in.at[f, y * n_dp + dp], direct_sem, f - staged, target)

    def back_copy(f, kd):
        target = place(kd, 0)
        return remote(result.at[f, target[0]], pool.at[f, core, y * n_dp + dp], back_sem, f, target)

    def back_direct(f, i):
        target = place(*far[i])
        return remote(result.at[f, target[0]], pool.at[f, core, y * n_dp + dp], back_direct_sem, f - backed, target)

    def ysend_copy(f, ky):
        piece = pool.at[f, core, pl.ds(y * n_dp, n_dp)]
        return remote(piece, piece, ysend_sem, f, place(0, ky))

    def forward_copy(f):
        return remote(pool.at[f, core], pool.at[f, core], fwd_sem, f, partner)

    n_far = len(far)

    router_copy = pltpu.make_async_copy(router_hbm, router, weight_sem.at[2])
    router_copy.start()
    spread_copy = pltpu.make_async_copy(spread_hbm, spread, weight_sem.at[3])
    spread_copy.start()
    up_copy = pltpu.make_async_copy(up_hbm.at[0], up, weight_sem.at[0])
    down_copy = pltpu.make_async_copy(down_hbm.at[0], down, weight_sem.at[1])

    def signal(target):
        pl.semaphore_signal(barrier, inc=1, device_id=target, device_id_type=MESH)

    barrier = pltpu.get_barrier_semaphore()
    for kd, ky in far:
        signal(place(kd, ky))
    for ky in range(n_y):
        signal((dp, lax.rem(y + ky, n_y) * CORES + other))

    for c in range(clips):
        token_copy(c).start()

    router_copy.wait()
    spread_copy.wait()
    routed[...] = jnp.dot(spread[...], router[...], preferred_element_type=F32).T.astype(BF16)

    @pl.loop(0, clips)
    def _(c):
        token_copy(c).wait()
        rows_of = pl.ds(pl.multiple_of(c * tok_dev, tok_dev), tok_dev)
        here = jnp.dot(tok[rows_of, :], routed[...], preferred_element_type=F32)
        flipped[...] = jnp.where(clip_rows((tok_dev, rows), c, per_expert, group, 1), here, flipped[...])

    up_copy.start()
    down_copy.start()
    logit[...] = flipped[...].T
    highest = jnp.max(logit[...], axis=1, keepdims=True)
    powers = jnp.exp(logit[...] - highest)
    total = jnp.sum(powers, axis=1, keepdims=True)
    lane = lax.broadcasted_iota(jnp.int32, (rows, 128), 1)
    stat[...] = jnp.where(lane == 0, highest, total).T[0:8, :]
    pl.semaphore_wait(barrier, len(far) + n_y)
    for k in range(1, n_ctx):
        stat_copy(k).start()
    powers = powers.astype(BF16)
    for c in range(clips):
        keep = jnp.where(clip_rows((rows, 128), c, per_expert, group), 1.0, 0.0).astype(BF16)
        for t in range(0, tok_dev, 128):
            diag[:, pl.ds(c * tok_dev + t, 128)] = powers[:, t : t + 128] * keep

    @pl.loop(0, chunks)
    def _(f):
        value = jnp.dot(diag[...], tok[:, lanes(f)], preferred_element_type=F32)
        part[f] = value.reshape(CORES, n_y * n_dp, group, width).astype(BF16)
        core_copy(f).start()

    await_bytes(stats_in, stat_sem.at[1])
    best = [stat[0:1, :]] + [stats_in[k, 0:1, :] for k in range(n_ctx - 1)]
    amount = [stat[1:2, :]] + [stats_in[k, 1:2, :] for k in range(n_ctx - 1)]
    top = functools.reduce(jnp.maximum, best)
    shrink = [jnp.exp(b - top) for b in best]
    whole = functools.reduce(jnp.add, [a * s for a, s in zip(amount, shrink)])
    theirs = jnp.where(core == 0, shrink[n_ctx - 1], shrink[1])
    sub = lax.broadcasted_iota(jnp.int32, (128, rows), 0)
    scales = jnp.where(sub == 0, shrink[0] / whole, theirs / whole).T
    columns[...] = scales.reshape(CORES, n_y * n_dp, group, 128)

    def merge(f):
        core_copy(f).wait_recv()
        scales = columns[core]
        mine, theirs = scales[:, :, 0:1], scales[:, :, 1:2]
        value = part[f, core].astype(F32) * mine + from_core[f].astype(F32) * theirs
        chip[f] = value.astype(BF16)

    @pl.loop(0, staged)
    def _(f):
        merge(f)
        for ky in range(1, n_y):
            y_copy(f, ky).start()

    @pl.loop(staged, chunks)
    def _(f):
        merge(f)
        rows_in[f, y * n_dp + dp] = chip[f, y * n_dp + dp]
        for i in range(len(far)):
            direct_copy(f, i).start()

    @pl.loop(0, staged)
    def _(f):
        await_bytes(from_y.at[f], y_sem.at[1 + f])
        value = chip[f, pl.ds(y * n_dp, n_dp)].astype(F32)
        for ky in range(1, n_y):
            value = value + from_y[f, ky - 1].astype(F32)
        slab[f] = value.astype(BF16)
        rows_in[f, dp] = slab[f, dp]
        for kd in range(1, n_dp):
            slab_copy(f, kd).start()

    blocks = logit[...].reshape(rows // group, group, tok_dev)
    peak = jnp.max(blocks, axis=0)

    def over_slots(values, reduce, neutral):
        out = values
        for c in range(clips):
            keep = clip_rows((group, tok_dev), c, per_expert, group)
            out = jnp.where(keep, reduce(jnp.where(keep, values, neutral), axis=0, keepdims=True), out)
        return out

    peak = over_slots(peak, jnp.max, -jnp.inf)
    powers = jnp.exp(blocks - peak[None])
    norm = over_slots(jnp.sum(powers, axis=0), jnp.sum, 0.0)
    combine_ref[...] = (powers / norm[None]).reshape(rows, tok_dev).T.astype(BF16)

    acc[...] = jnp.zeros_like(acc)
    up_copy.wait()

    def expand(f, value):
        value = value.reshape(n_dp * group, width).astype(BF16)
        row0 = pl.multiple_of(f * width, width)
        acc[...] += jnp.dot(value, up[pl.ds(row0, width), :], preferred_element_type=F32)

    @pl.loop(staged, chunks)
    def _(f):
        await_bytes(rows_in.at[f, pl.ds(0, n_far)], direct_sem.at[1 + f - staged])
        value = rows_in[f, pl.ds(0, n_dp)].astype(F32)
        for k in range(1, n_y):
            value = value + rows_in[f, pl.ds(k * n_dp, n_dp)].astype(F32)
        expand(f, value)

    @pl.loop(0, staged)
    def _(f):
        await_bytes(rows_in.at[f, pl.ds(0, n_dp - 1)], slab_sem.at[1 + f])
        expand(f, rows_in[f, pl.ds(0, n_dp)].astype(F32))

    value = acc[...]
    hidden[...] = (0.5 * value * (1.0 + lax.erf(value * np.float32(np.sqrt(0.5))))).astype(BF16)
    down_copy.wait()

    def contract(f):
        value = jnp.dot(hidden[...], down[:, lanes(f)], preferred_element_type=F32)
        result[f] = value.reshape(n_dp, group, width).astype(BF16)
        pool[f, core, y * n_dp + dp] = result[f, dp]

    @pl.loop(0, backed)
    def _(f):
        contract(f)
        for kd in range(1, n_dp):
            back_copy(f, kd).start()

    @pl.loop(backed, chunks)
    def _(f):
        contract(f)
        for i in range(len(far)):
            back_direct(f, i).start()

    @pl.loop(0, backed)
    def _(f):
        await_bytes(result.at[f, pl.ds(0, n_dp - 1)], back_sem.at[1 + f])
        for ky in range(1, n_y):
            ysend_copy(f, ky).start()

    @pl.loop(0, backed)
    def _(f):
        await_bytes(from_y.at[f], ysend_sem.at[1 + f])
        forward_copy(f).start()

    @pl.loop(backed, chunks)
    def _(f):
        await_bytes(pool.at[f, core, pl.ds(0, n_far)], back_direct_sem.at[1 + f - backed])
        forward_copy(f).start()

    @pl.loop(0, chunks)
    def _(f):
        forward_copy(f).wait_recv()
        gathered_ref[f] = pool[f].astype(F32).reshape(rows, width).astype(BF16)

    await_bytes(stats_in, stat_sem.at[0])
    await_bytes(from_core, core_sem.at[0])
    await_bytes(pool.at[:, core], fwd_sem.at[0])
    if staged:
        await_bytes(from_y.at[pl.ds(0, staged)], y_sem.at[0])
        await_bytes(slab.at[pl.ds(0, staged), pl.ds(0, n_dp - 1)], slab_sem.at[0])
    if staged < chunks:
        await_bytes(chip.at[pl.ds(0, chunks - staged), pl.ds(0, n_far)], direct_sem.at[0])
    if backed:
        await_bytes(from_y.at[pl.ds(0, backed)], ysend_sem.at[0])
        await_bytes(result.at[pl.ds(0, backed), pl.ds(0, n_dp - 1)], back_sem.at[0])
    if backed < chunks:
        await_bytes(chip.at[pl.ds(0, chunks - backed), pl.ds(0, n_far)], back_direct_sem.at[0])


def mix(clips, per_expert, chunks, width, parts, combine_ref, gathered_ref, out_hbm, stage, sem):
    tok_dev = combine_ref.shape[0]
    group = clips * per_expert
    size = tok_dev // parts
    copies = []
    for c in range(clips):
        for p in range(parts):
            piece = combine_ref[pl.ds(p * size, size), :]
            keep = clip_rows(piece.shape, c, per_expert, group, 1)
            weights = jnp.where(keep, piece.astype(F32), 0.0).astype(BF16)
            here = pl.ds(p * size, size)
            for f in range(chunks):
                stage[c, here, pl.ds(f * width, width)] = jnp.dot(
                    weights, gathered_ref[f], preferred_element_type=F32
                ).astype(BF16)
            copy = pltpu.make_async_copy(stage.at[c, here], out_hbm.at[c, here], sem.at[c, p])
            copy.start()
            copies.append(copy)
    for copy in copies:
        copy.wait()


def shards(n_dp, n_ctx, tokens, router, expert_up, expert_down):
    clips, tok_dev, feature = tokens.shape
    slots = router.shape[1]
    hidden = expert_up.shape[2]
    per_expert = slots // (n_dp * n_ctx)
    n_y = n_ctx // CORES
    group = clips * per_expert
    rows = n_dp * n_ctx * group
    width = 256
    parts = 2
    chunks = feature // width
    order = np.arange(slots).reshape(n_dp, n_y, CORES, 1, per_expert).transpose(2, 1, 0, 3, 4)
    order = np.broadcast_to(order, (CORES, n_y, n_dp, clips, per_expert)).reshape(-1)
    spread = jnp.asarray(order[:, None] == np.arange(slots)[None, :], BF16)
    staged, backed = 2, 2
    dims = (n_dp, n_ctx, clips, tok_dev, per_expert, chunks, width, staged, backed)
    vmem = pl.BlockSpec(memory_space=pltpu.VMEM)
    hbm = pl.BlockSpec(memory_space=pl.ANY)
    piece = (n_dp, group, width)
    dma = pltpu.SemaphoreType.DMA
    gathered, combine = pl.pallas_call(
        functools.partial(exchange, dims),
        out_shape=(
            pltpu.VMEM((chunks, rows, width), BF16),
            pltpu.VMEM((tok_dev, rows), BF16),
        ),
        in_specs=[hbm] * 5,
        out_specs=(vmem, vmem),
        scratch_shapes=[
            pltpu.VMEM((clips * tok_dev, feature), BF16),
            pltpu.VMEM((slots, feature), BF16),
            pltpu.VMEM((rows, slots), BF16),
            pltpu.VMEM((feature, rows), BF16),
            pltpu.VMEM((feature, hidden), BF16),
            pltpu.VMEM((hidden, feature), BF16),
            pltpu.VMEM((tok_dev, rows), F32),
            pltpu.VMEM((rows, tok_dev), F32),
            pltpu.VMEM((rows, clips * tok_dev), BF16),
            pltpu.VMEM((n_dp * group, hidden), F32),
            pltpu.VMEM((n_dp * group, hidden), BF16),
            pltpu.VMEM((chunks, CORES, n_y * n_dp, group, width), BF16),
            pltpu.VMEM((chunks, n_y * n_dp, group, width), BF16),
            pltpu.VMEM((chunks, n_y * n_dp, group, width), BF16),
            pltpu.VMEM((chunks, n_y - 1) + piece, BF16),
            pltpu.VMEM((chunks,) + piece, BF16),
            pltpu.VMEM((chunks, n_y * n_dp, group, width), BF16),
            pltpu.VMEM((chunks,) + piece, BF16),
            pltpu.VMEM((chunks, CORES, n_y * n_dp, group, width), BF16),
            pltpu.VMEM((8, rows), F32),
            pltpu.VMEM((n_ctx - 1, 8, rows), F32),
            pltpu.VMEM((CORES, n_y * n_dp, group, 128), F32),
            dma((clips,)),
            dma((4,)),
            dma((2,)),
            dma((1 + chunks,)),
            dma((1 + staged,)),
            dma((1 + staged,)),
            dma((1 + chunks - staged,)),
            dma((1 + backed,)),
            dma((1 + chunks - backed,)),
            dma((1 + backed,)),
            dma((1 + chunks,)),
        ],
        compiler_params=pltpu.CompilerParams(collective_id=0, has_side_effects=True, vmem_limit_bytes=58 * MIB),
        name="exchange",
    )(tokens, router.T, spread, expert_up, expert_down)
    gathered = pltpu.with_memory_space_constraint(gathered, pltpu.VMEM)
    combine = pltpu.with_memory_space_constraint(combine, pltpu.VMEM)
    return pl.pallas_call(
        functools.partial(mix, clips, per_expert, chunks, width, parts),
        out_shape=jax.ShapeDtypeStruct(tokens.shape, BF16),
        in_specs=[vmem, vmem],
        out_specs=hbm,
        scratch_shapes=[pltpu.VMEM(tokens.shape, BF16), dma((clips, parts))],
        compiler_params=pltpu.CompilerParams(vmem_limit_bytes=32 * MIB),
        name="mix",
    )(combine, gathered)


def solution(mesh):
    in_specs = (
        P("dp", "ctx", None),
        P(),
        P(("dp", "ctx"), None, None),
        P(("dp", "ctx"), None, None),
    )
    out_specs = P("dp", "ctx", None)
    body = functools.partial(shards, mesh.shape["dp"], mesh.shape["ctx"])
    return jax.shard_map(body, mesh=mesh, in_specs=in_specs, out_specs=out_specs, check_vma=False)
```

```python
import functools

import jax
import jax.numpy as jnp
import numpy as np
from jax import lax
from jax.experimental import pallas as pl
from jax.experimental.pallas import tpu as pltpu
from jax.sharding import PartitionSpec as P

MESH = pl.DeviceIdType.MESH
CORES = 2
F32 = jnp.float32
BF16 = jnp.bfloat16
MIB = 2**20


def clip_rows(shape, clip, per_clip, group, dim=0):
    place = lax.rem(lax.broadcasted_iota(jnp.int32, shape, dim), group)
    return (place >= clip * per_clip) & (place < (clip + 1) * per_clip)


def exchange(
    dims, tok_hbm, router_hbm, spread_hbm, up_hbm, down_hbm, gathered_ref, combine_ref,
    tok, router, spread, routed, up, down, flipped, logit, diag, acc, hidden, part, from_core, chip, from_y, slab,
    rows_in, result, pool, stat, stats_in, columns,
    tok_sem, weight_sem, stat_sem, core_sem, y_sem, slab_sem, direct_sem, back_sem, back_near_sem, back_direct_sem,
    ysend_sem, fwd_sem,
):
    n_dp, n_ctx, clips, tok_dev, per_expert, chunks, width, staged, backed = dims
    n_y = n_ctx // CORES
    group = clips * per_expert
    rows = n_dp * n_ctx * group
    half = rows // CORES
    dp = lax.axis_index("dp")
    ctx = lax.axis_index("ctx")
    y = ctx // CORES
    core = ctx % CORES
    other = 1 - core
    partner = (dp, y * CORES + other)
    far = [(kd, ky) for kd in range(n_dp) for ky in range(n_y) if (kd, ky) != (0, 0)]
    side = n_dp // 2
    near0 = (dp // side) * side
    far0 = (1 - dp // side) * side
    near = [(kd, ky) for kd in range(side) for ky in range(n_y) if (kd, ky) != (0, 0)]

    def place(kd, ky):
        return (lax.rem(dp + kd, n_dp), lax.rem(y + ky, n_y) * CORES + core)

    def lanes(f):
        return pl.ds(pl.multiple_of(f * width, width), width)

    def remote(src, dst, sems, index, target):
        return pltpu.make_async_remote_copy(
            src_ref=src, dst_ref=dst, send_sem=sems.at[0], recv_sem=sems.at[1 + index],
            device_id=target, device_id_type=MESH,
        )

    def await_bytes(ref, sem):
        pltpu.make_async_copy(ref, ref, sem).wait()

    def token_copy(c):
        there = tok.at[pl.ds(pl.multiple_of(c * tok_dev, tok_dev), tok_dev)]
        return pltpu.make_async_copy(tok_hbm.at[c], there, tok_sem.at[c])

    def stat_copy(k):
        return remote(stat, stats_in.at[k - 1], stat_sem, 0, (dp, lax.rem(ctx + k, n_ctx)))

    def core_copy(f):
        return remote(part.at[f, other], from_core.at[f], core_sem, f, partner)

    def y_copy(f, ky):
        target = place(0, ky)
        src = chip.at[f, pl.ds(lax.rem(y + ky, n_y) * n_dp + far0, side)]
        return remote(src, from_y.at[f, ky - 1], y_sem, f, target)

    def near_place(kd, ky):
        return (near0 + lax.rem(dp - near0 + kd, side), lax.rem(y + ky, n_y) * CORES + core)

    def far_place(kd):
        return (far0 + lax.rem(dp - near0 + kd, side), ctx)

    def slab_copy(f, kd):
        target = far_place(kd)
        return remote(slab.at[f, target[0] - far0], rows_in.at[f, dp], slab_sem, f, target)

    def near_copy(f, i):
        target = near_place(*near[i])
        src = chip.at[f, lax.rem(y + near[i][1], n_y) * n_dp + target[0]]
        return remote(src, rows_in.at[f, y * n_dp + dp], slab_sem, f, target)

    def direct_copy(f, i):
        target = place(*far[i])
        src = chip.at[f, lax.rem(y + far[i][1], n_y) * n_dp + target[0]]
        return remote(src, rows_in.at[f, y * n_dp + dp], direct_sem, f - staged, target)

    def back_copy(f, kd):
        target = far_place(kd)
        return remote(result.at[f, target[0]], pool.at[f, core, y * n_dp + dp], back_sem, f, target)

    def back_near(f, i):
        target = near_place(*near[i])
        return remote(result.at[f, target[0]], pool.at[f, core, y * n_dp + dp], back_near_sem, f, target)

    def back_direct(f, i):
        target = place(*far[i])
        return remote(result.at[f, target[0]], pool.at[f, core, y * n_dp + dp], back_direct_sem, f - backed, target)

    def ysend_copy(f, ky):
        piece = pool.at[f, core, pl.ds(y * n_dp + far0, side)]
        return remote(piece, piece, ysend_sem, f, place(0, ky))

    def forward_copy(f):
        return remote(pool.at[f, core], pool.at[f, core], fwd_sem, f, partner)

    n_far = len(far)

    router_copy = pltpu.make_async_copy(router_hbm, router, weight_sem.at[2])
    router_copy.start()
    spread_copy = pltpu.make_async_copy(spread_hbm, spread, weight_sem.at[3])
    spread_copy.start()
    up_copy = pltpu.make_async_copy(up_hbm.at[0], up, weight_sem.at[0])
    down_copy = pltpu.make_async_copy(down_hbm.at[0], down, weight_sem.at[1])

    def signal(target):
        pl.semaphore_signal(barrier, inc=1, device_id=target, device_id_type=MESH)

    barrier = pltpu.get_barrier_semaphore()
    for kd, ky in far:
        signal(place(kd, ky))
    for ky in range(n_y):
        signal((dp, lax.rem(y + ky, n_y) * CORES + other))

    for c in range(clips):
        token_copy(c).start()

    router_copy.wait()
    spread_copy.wait()
    routed[...] = jnp.dot(spread[...], router[...], preferred_element_type=F32).T.astype(BF16)

    @pl.loop(0, clips)
    def _(c):
        token_copy(c).wait()
        rows_of = pl.ds(pl.multiple_of(c * tok_dev, tok_dev), tok_dev)
        here = jnp.dot(tok[rows_of, :], routed[...], preferred_element_type=F32)
        flipped[...] = jnp.where(clip_rows((tok_dev, rows), c, per_expert, group, 1), here, flipped[...])

    up_copy.start()
    down_copy.start()
    logit[...] = flipped[...].T
    highest = jnp.max(logit[...], axis=1, keepdims=True)
    powers = jnp.exp(logit[...] - highest)
    total = jnp.sum(powers, axis=1, keepdims=True)
    lane = lax.broadcasted_iota(jnp.int32, (rows, 128), 1)
    stat[...] = jnp.where(lane == 0, highest, total).T[0:8, :]
    pl.semaphore_wait(barrier, len(far) + n_y)
    for k in range(1, n_ctx):
        stat_copy(k).start()
    powers = powers.astype(BF16)
    for c in range(clips):
        keep = jnp.where(clip_rows((rows, 128), c, per_expert, group), 1.0, 0.0).astype(BF16)
        for t in range(0, tok_dev, 128):
            diag[:, pl.ds(c * tok_dev + t, 128)] = powers[:, t : t + 128] * keep

    @pl.loop(0, chunks)
    def _(f):
        value = jnp.dot(diag[...], tok[:, lanes(f)], preferred_element_type=F32)
        part[f] = value.reshape(CORES, n_y * n_dp, group, width).astype(BF16)
        core_copy(f).start()

    await_bytes(stats_in, stat_sem.at[1])
    best = [stat[0:1, :]] + [stats_in[k, 0:1, :] for k in range(n_ctx - 1)]
    amount = [stat[1:2, :]] + [stats_in[k, 1:2, :] for k in range(n_ctx - 1)]
    top = functools.reduce(jnp.maximum, best)
    shrink = [jnp.exp(b - top) for b in best]
    whole = functools.reduce(jnp.add, [a * s for a, s in zip(amount, shrink)])
    theirs = jnp.where(core == 0, shrink[n_ctx - 1], shrink[1])

    def to_rows(value):
        value = jnp.where(core == 0, value[:, :half], value[:, half:])
        return jnp.broadcast_to(value, (128, half)).T.reshape(n_y * n_dp, group, 128)

    columns[0] = to_rows(shrink[0] / whole)
    columns[1] = to_rows(theirs / whole)

    def merge(f):
        core_copy(f).wait_recv()
        mine = jnp.concatenate([columns[0]] * (width // 128), axis=-1)
        theirs = jnp.concatenate([columns[1]] * (width // 128), axis=-1)
        value = part[f, core].astype(F32) * mine + from_core[f].astype(F32) * theirs
        chip[f] = value.astype(BF16)

    @pl.loop(0, staged)
    def _(f):
        merge(f)
        for ky in range(1, n_y):
            y_copy(f, ky).start()

    @pl.loop(staged, chunks)
    def _(f):
        merge(f)
        rows_in[f, y * n_dp + dp] = chip[f, y * n_dp + dp]
        for i in range(len(far)):
            direct_copy(f, i).start()

    @pl.loop(0, staged)
    def _(f):
        rows_in[f, y * n_dp + dp] = chip[f, y * n_dp + dp]
        for i in range(len(near)):
            near_copy(f, i).start()

    @pl.loop(0, staged)
    def _(f):
        await_bytes(from_y.at[f], y_sem.at[1 + f])
        value = chip[f, pl.ds(y * n_dp + far0, side)].astype(F32)
        for ky in range(1, n_y):
            value = value + from_y[f, ky - 1].astype(F32)
        slab[f] = value.astype(BF16)
        for kd in range(side):
            slab_copy(f, kd).start()

    blocks = logit[...].reshape(rows // group, group, tok_dev)
    peak = jnp.max(blocks, axis=0)

    def over_slots(values, reduce, neutral):
        out = values
        for c in range(clips):
            keep = clip_rows((group, tok_dev), c, per_expert, group)
            out = jnp.where(keep, reduce(jnp.where(keep, values, neutral), axis=0, keepdims=True), out)
        return out

    peak = over_slots(peak, jnp.max, -jnp.inf)
    powers = jnp.exp(blocks - peak[None])
    norm = over_slots(jnp.sum(powers, axis=0), jnp.sum, 0.0)
    combine_ref[...] = (powers / norm[None]).reshape(rows, tok_dev).T.astype(BF16)

    acc[...] = jnp.zeros_like(acc)
    up_copy.wait()

    def expand(f, value):
        value = value.reshape(n_dp * group, width).astype(BF16)
        row0 = pl.multiple_of(f * width, width)
        acc[...] += jnp.dot(value, up[pl.ds(row0, width), :], preferred_element_type=F32)

    @pl.loop(staged, chunks)
    def _(f):
        await_bytes(rows_in.at[f, pl.ds(0, n_far)], direct_sem.at[1 + f - staged])
        value = rows_in[f, pl.ds(0, n_dp)].astype(F32)
        for k in range(1, n_y):
            value = value + rows_in[f, pl.ds(k * n_dp, n_dp)].astype(F32)
        expand(f, value)

    @pl.loop(0, staged)
    def _(f):
        await_bytes(rows_in.at[f, pl.ds(0, side + len(near))], slab_sem.at[1 + f])
        value = rows_in[f, pl.ds(near0, side)].astype(F32)
        for k in range(1, n_y):
            value = value + rows_in[f, pl.ds(k * n_dp + near0, side)].astype(F32)
        rows_in[f, pl.ds(near0, side)] = value.astype(BF16)
        expand(f, rows_in[f, pl.ds(0, n_dp)].astype(F32))

    value = acc[...]
    hidden[...] = (0.5 * value * (1.0 + lax.erf(value * np.float32(np.sqrt(0.5))))).astype(BF16)
    down_copy.wait()

    def contract(f):
        value = jnp.dot(hidden[...], down[:, lanes(f)], preferred_element_type=F32)
        result[f] = value.reshape(n_dp, group, width).astype(BF16)
        pool[f, core, y * n_dp + dp] = result[f, dp]

    @pl.loop(0, backed)
    def _(f):
        contract(f)
        for kd in range(side):
            back_copy(f, kd).start()
        for i in range(len(near)):
            back_near(f, i).start()

    @pl.loop(backed, chunks)
    def _(f):
        contract(f)
        for i in range(len(far)):
            back_direct(f, i).start()

    @pl.loop(0, backed)
    def _(f):
        await_bytes(result.at[f, pl.ds(0, side)], back_sem.at[1 + f])
        for ky in range(1, n_y):
            ysend_copy(f, ky).start()

    @pl.loop(0, backed)
    def _(f):
        await_bytes(pool.at[f, core, pl.ds(0, len(near))], back_near_sem.at[1 + f])
        await_bytes(from_y.at[f], ysend_sem.at[1 + f])
        forward_copy(f).start()

    @pl.loop(backed, chunks)
    def _(f):
        await_bytes(pool.at[f, core, pl.ds(0, n_far)], back_direct_sem.at[1 + f - backed])
        forward_copy(f).start()

    @pl.loop(0, chunks)
    def _(f):
        forward_copy(f).wait_recv()
        gathered_ref[f] = pool[f].astype(F32).reshape(rows, width).astype(BF16)

    await_bytes(stats_in, stat_sem.at[0])
    await_bytes(from_core, core_sem.at[0])
    await_bytes(pool.at[:, core], fwd_sem.at[0])
    if staged:
        await_bytes(from_y.at[pl.ds(0, staged)], y_sem.at[0])
        await_bytes(chip.at[pl.ds(0, staged), pl.ds(0, side + len(near))], slab_sem.at[0])
    if staged < chunks:
        await_bytes(chip.at[pl.ds(0, chunks - staged), pl.ds(0, n_far)], direct_sem.at[0])
    if backed:
        await_bytes(from_y.at[pl.ds(0, backed)], ysend_sem.at[0])
        await_bytes(result.at[pl.ds(0, backed), pl.ds(0, side)], back_sem.at[0])
        await_bytes(chip.at[pl.ds(0, backed), pl.ds(0, len(near))], back_near_sem.at[0])
    if backed < chunks:
        await_bytes(chip.at[pl.ds(0, chunks - backed), pl.ds(0, n_far)], back_direct_sem.at[0])


def mix(clips, per_expert, chunks, width, parts, combine_ref, gathered_ref, out_hbm, stage, sem):
    tok_dev = combine_ref.shape[0]
    group = clips * per_expert
    size = tok_dev // parts
    copies = []
    for c in range(clips):
        for p in range(parts):
            piece = combine_ref[pl.ds(p * size, size), :]
            keep = clip_rows(piece.shape, c, per_expert, group, 1)
            weights = jnp.where(keep, piece.astype(F32), 0.0).astype(BF16)
            here = pl.ds(p * size, size)
            for f in range(chunks):
                stage[c, here, pl.ds(f * width, width)] = jnp.dot(
                    weights, gathered_ref[f], preferred_element_type=F32
                ).astype(BF16)
            copy = pltpu.make_async_copy(stage.at[c, here], out_hbm.at[c, here], sem.at[c, p])
            copy.start()
            copies.append(copy)
    for copy in copies:
        copy.wait()


def shards(n_dp, n_ctx, tokens, router, expert_up, expert_down):
    clips, tok_dev, feature = tokens.shape
    slots = router.shape[1]
    hidden = expert_up.shape[2]
    per_expert = slots // (n_dp * n_ctx)
    n_y = n_ctx // CORES
    group = clips * per_expert
    rows = n_dp * n_ctx * group
    width = 256
    parts = 4
    chunks = feature // width
    order = np.arange(slots).reshape(n_dp, n_y, CORES, 1, per_expert).transpose(2, 1, 0, 3, 4)
    order = np.broadcast_to(order, (CORES, n_y, n_dp, clips, per_expert)).reshape(-1)
    spread = jnp.asarray(order[:, None] == np.arange(slots)[None, :], BF16)
    staged, backed = 3, 2
    dims = (n_dp, n_ctx, clips, tok_dev, per_expert, chunks, width, staged, backed)
    vmem = pl.BlockSpec(memory_space=pltpu.VMEM)
    hbm = pl.BlockSpec(memory_space=pl.ANY)
    piece = (n_dp, group, width)
    dma = pltpu.SemaphoreType.DMA
    gathered, combine = pl.pallas_call(
        functools.partial(exchange, dims),
        out_shape=(
            pltpu.VMEM((chunks, rows, width), BF16),
            pltpu.VMEM((tok_dev, rows), BF16),
        ),
        in_specs=[hbm] * 5,
        out_specs=(vmem, vmem),
        scratch_shapes=[
            pltpu.VMEM((clips * tok_dev, feature), BF16),
            pltpu.VMEM((slots, feature), BF16),
            pltpu.VMEM((rows, slots), BF16),
            pltpu.VMEM((feature, rows), BF16),
            pltpu.VMEM((feature, hidden), BF16),
            pltpu.VMEM((hidden, feature), BF16),
            pltpu.VMEM((tok_dev, rows), F32),
            pltpu.VMEM((rows, tok_dev), F32),
            pltpu.VMEM((rows, clips * tok_dev), BF16),
            pltpu.VMEM((n_dp * group, hidden), F32),
            pltpu.VMEM((n_dp * group, hidden), BF16),
            pltpu.VMEM((chunks, CORES, n_y * n_dp, group, width), BF16),
            pltpu.VMEM((chunks, n_y * n_dp, group, width), BF16),
            pltpu.VMEM((chunks, n_y * n_dp, group, width), BF16),
            pltpu.VMEM((chunks, n_y - 1, n_dp // 2, group, width), BF16),
            pltpu.VMEM((chunks, n_dp // 2, group, width), BF16),
            pltpu.VMEM((chunks, n_y * n_dp, group, width), BF16),
            pltpu.VMEM((chunks,) + piece, BF16),
            pltpu.VMEM((chunks, CORES, n_y * n_dp, group, width), BF16),
            pltpu.VMEM((8, rows), F32),
            pltpu.VMEM((n_ctx - 1, 8, rows), F32),
            pltpu.VMEM((CORES, n_y * n_dp, group, 128), F32),
            dma((clips,)),
            dma((4,)),
            dma((2,)),
            dma((1 + chunks,)),
            dma((1 + staged,)),
            dma((1 + staged,)),
            dma((1 + chunks - staged,)),
            dma((1 + backed,)),
            dma((1 + backed,)),
            dma((1 + chunks - backed,)),
            dma((1 + backed,)),
            dma((1 + chunks,)),
        ],
        compiler_params=pltpu.CompilerParams(collective_id=0, has_side_effects=True, vmem_limit_bytes=58 * MIB),
        name="exchange",
    )(tokens, router.T, spread, expert_up, expert_down)
    gathered = pltpu.with_memory_space_constraint(gathered, pltpu.VMEM)
    combine = pltpu.with_memory_space_constraint(combine, pltpu.VMEM)
    return pl.pallas_call(
        functools.partial(mix, clips, per_expert, chunks, width, parts),
        out_shape=jax.ShapeDtypeStruct(tokens.shape, BF16),
        in_specs=[vmem, vmem],
        out_specs=hbm,
        scratch_shapes=[pltpu.VMEM(tokens.shape, BF16), dma((clips, parts))],
        compiler_params=pltpu.CompilerParams(vmem_limit_bytes=32 * MIB),
        name="mix",
    )(combine, gathered)


def solution(mesh):
    in_specs = (
        P("dp", "ctx", None),
        P(),
        P(("dp", "ctx"), None, None),
        P(("dp", "ctx"), None, None),
    )
    out_specs = P("dp", "ctx", None)
    body = functools.partial(shards, mesh.shape["dp"], mesh.shape["ctx"])
    return jax.shard_map(body, mesh=mesh, in_specs=in_specs, out_specs=out_specs, check_vma=False)
```

```python
import functools

import jax
import jax.numpy as jnp
import numpy as np
from jax import lax
from jax.experimental import pallas as pl
from jax.experimental.pallas import tpu as pltpu
from jax.sharding import PartitionSpec as P

MESH = pl.DeviceIdType.MESH
CORES = 2
F32 = jnp.float32
BF16 = jnp.bfloat16
MIB = 2**20


def clip_rows(shape, clip, per_clip, group, dim=0):
    place = lax.rem(lax.broadcasted_iota(jnp.int32, shape, dim), group)
    return (place >= clip * per_clip) & (place < (clip + 1) * per_clip)


def exchange(
    dims, tok_hbm, router_hbm, spread_hbm, up_hbm, down_hbm, gathered_ref, combine_ref,
    tok, router, spread, routed, up, down, flipped, logit, diag, acc, hidden, part, from_core, chip, from_y, slab,
    rows_in, result, pool, stat, stats_in, columns,
    tok_sem, weight_sem, stat_sem, core_sem, y_sem, slab_sem, direct_sem, back_sem, back_near_sem, back_direct_sem,
    ysend_sem, fwd_sem,
):
    n_dp, n_ctx, clips, tok_dev, per_expert, chunks, width, staged, backed = dims
    n_y = n_ctx // CORES
    group = clips * per_expert
    rows = n_dp * n_ctx * group
    half = rows // CORES
    dp = lax.axis_index("dp")
    ctx = lax.axis_index("ctx")
    y = ctx // CORES
    core = ctx % CORES
    other = 1 - core
    partner = (dp, y * CORES + other)
    far = [(kd, ky) for kd in range(n_dp) for ky in range(n_y) if (kd, ky) != (0, 0)]
    side = n_dp // 2
    near0 = (dp // side) * side
    far0 = (1 - dp // side) * side
    near = [(kd, ky) for kd in range(side) for ky in range(n_y) if (kd, ky) != (0, 0)]

    def place(kd, ky):
        return (lax.rem(dp + kd, n_dp), lax.rem(y + ky, n_y) * CORES + core)

    def lanes(f):
        return pl.ds(pl.multiple_of(f * width, width), width)

    def remote(src, dst, sems, index, target):
        return pltpu.make_async_remote_copy(
            src_ref=src, dst_ref=dst, send_sem=sems.at[0], recv_sem=sems.at[1 + index],
            device_id=target, device_id_type=MESH,
        )

    def await_bytes(ref, sem):
        pltpu.make_async_copy(ref, ref, sem).wait()

    def token_copy(c):
        there = tok.at[pl.ds(pl.multiple_of(c * tok_dev, tok_dev), tok_dev)]
        return pltpu.make_async_copy(tok_hbm.at[c], there, tok_sem.at[c])

    def stat_copy(k):
        return remote(stat, stats_in.at[k - 1], stat_sem, 0, (dp, lax.rem(ctx + k, n_ctx)))

    def core_copy(f):
        return remote(part.at[f, other], from_core.at[f], core_sem, f, partner)

    def y_copy(f, ky):
        target = place(0, ky)
        src = chip.at[f, pl.ds(lax.rem(y + ky, n_y) * n_dp + far0, side)]
        return remote(src, from_y.at[f, ky - 1], y_sem, f, target)

    def near_place(kd, ky):
        return (near0 + lax.rem(dp - near0 + kd, side), lax.rem(y + ky, n_y) * CORES + core)

    def far_place(kd):
        return (far0 + lax.rem(dp - near0 + kd, side), ctx)

    def slab_copy(f, kd):
        target = far_place(kd)
        return remote(slab.at[f, target[0] - far0], rows_in.at[f, dp], slab_sem, f, target)

    def near_copy(f, i):
        target = near_place(*near[i])
        src = chip.at[f, lax.rem(y + near[i][1], n_y) * n_dp + target[0]]
        return remote(src, rows_in.at[f, y * n_dp + dp], slab_sem, f, target)

    def direct_copy(f, i):
        target = place(*far[i])
        src = chip.at[f, lax.rem(y + far[i][1], n_y) * n_dp + target[0]]
        return remote(src, rows_in.at[f, y * n_dp + dp], direct_sem, f - staged, target)

    def back_copy(f, kd):
        target = far_place(kd)
        return remote(result.at[f, target[0]], pool.at[f, core, y * n_dp + dp], back_sem, f, target)

    def back_near(i):
        target = near_place(*near[i])
        some = pl.ds(0, backed)
        return remote(result.at[some, target[0]], pool.at[some, core, y * n_dp + dp], back_near_sem, 0, target)

    rest = pl.ds(backed, chunks - backed)

    def back_direct(i):
        target = place(*far[i])
        return remote(result.at[rest, target[0]], pool.at[rest, core, y * n_dp + dp], back_direct_sem, 0, target)

    def ysend_copy(f, ky):
        piece = pool.at[f, core, pl.ds(y * n_dp + far0, side)]
        return remote(piece, piece, ysend_sem, f, place(0, ky))

    def forward_copy(f):
        return remote(pool.at[f, core], pool.at[f, core], fwd_sem, f, partner)

    n_far = len(far)

    router_copy = pltpu.make_async_copy(router_hbm, router, weight_sem.at[2])
    router_copy.start()
    spread_copy = pltpu.make_async_copy(spread_hbm, spread, weight_sem.at[3])
    spread_copy.start()
    up_copy = pltpu.make_async_copy(up_hbm.at[0], up, weight_sem.at[0])
    down_copy = pltpu.make_async_copy(down_hbm.at[0], down, weight_sem.at[1])

    def signal(target):
        pl.semaphore_signal(barrier, inc=1, device_id=target, device_id_type=MESH)

    barrier = pltpu.get_barrier_semaphore()
    for kd, ky in far:
        signal(place(kd, ky))
    for ky in range(n_y):
        signal((dp, lax.rem(y + ky, n_y) * CORES + other))

    for c in range(clips):
        token_copy(c).start()

    router_copy.wait()
    spread_copy.wait()
    routed[...] = jnp.dot(spread[...], router[...], preferred_element_type=F32).T.astype(BF16)

    @pl.loop(0, clips)
    def _(c):
        token_copy(c).wait()
        rows_of = pl.ds(pl.multiple_of(c * tok_dev, tok_dev), tok_dev)
        here = jnp.dot(tok[rows_of, :], routed[...], preferred_element_type=F32)
        flipped[...] = jnp.where(clip_rows((tok_dev, rows), c, per_expert, group, 1), here, flipped[...])

    up_copy.start()
    down_copy.start()
    logit[...] = flipped[...].T
    highest = jnp.max(logit[...], axis=1, keepdims=True)
    powers = jnp.exp(logit[...] - highest)
    total = jnp.sum(powers, axis=1, keepdims=True)
    lane = lax.broadcasted_iota(jnp.int32, (rows, 128), 1)
    stat[...] = jnp.where(lane == 0, highest, total).T[0:8, :]
    pl.semaphore_wait(barrier, len(far) + n_y)
    for k in range(1, n_ctx):
        stat_copy(k).start()
    powers = powers.astype(BF16)
    for c in range(clips):
        keep = jnp.where(clip_rows((rows, 128), c, per_expert, group), 1.0, 0.0).astype(BF16)
        for t in range(0, tok_dev, 128):
            diag[:, pl.ds(c * tok_dev + t, 128)] = powers[:, t : t + 128] * keep

    @pl.loop(0, chunks)
    def _(f):
        value = jnp.dot(diag[...], tok[:, lanes(f)], preferred_element_type=F32)
        part[f] = value.reshape(CORES, n_y * n_dp, group, width).astype(BF16)
        core_copy(f).start()

    await_bytes(stats_in, stat_sem.at[1])
    best = [stat[0:1, :]] + [stats_in[k, 0:1, :] for k in range(n_ctx - 1)]
    amount = [stat[1:2, :]] + [stats_in[k, 1:2, :] for k in range(n_ctx - 1)]
    top = functools.reduce(jnp.maximum, best)
    shrink = [jnp.exp(b - top) for b in best]
    whole = functools.reduce(jnp.add, [a * s for a, s in zip(amount, shrink)])
    theirs = jnp.where(core == 0, shrink[n_ctx - 1], shrink[1])

    def to_rows(value):
        value = jnp.where(core == 0, value[:, :half], value[:, half:])
        return jnp.broadcast_to(value, (128, half)).T.reshape(n_y * n_dp, group, 128)

    columns[0] = to_rows(shrink[0] / whole)
    columns[1] = to_rows(theirs / whole)

    def merge(f):
        core_copy(f).wait_recv()
        mine = jnp.concatenate([columns[0]] * (width // 128), axis=-1)
        theirs = jnp.concatenate([columns[1]] * (width // 128), axis=-1)
        value = part[f, core].astype(F32) * mine + from_core[f].astype(F32) * theirs
        chip[f] = value.astype(BF16)

    @pl.loop(0, staged)
    def _(f):
        merge(f)
        for ky in range(1, n_y):
            y_copy(f, ky).start()

    @pl.loop(staged, chunks)
    def _(f):
        merge(f)
        rows_in[f, y * n_dp + dp] = chip[f, y * n_dp + dp]
        for i in range(len(far)):
            direct_copy(f, i).start()

    @pl.loop(0, staged)
    def _(f):
        rows_in[f, y * n_dp + dp] = chip[f, y * n_dp + dp]
        for i in range(len(near)):
            near_copy(f, i).start()

    @pl.loop(0, staged)
    def _(f):
        await_bytes(from_y.at[f], y_sem.at[1 + f])
        value = chip[f, pl.ds(y * n_dp + far0, side)].astype(F32)
        for ky in range(1, n_y):
            value = value + from_y[f, ky - 1].astype(F32)
        slab[f] = value.astype(BF16)
        for kd in range(side):
            slab_copy(f, kd).start()

    blocks = logit[...].reshape(rows // group, group, tok_dev)
    peak = jnp.max(blocks, axis=0)

    def over_slots(values, reduce, neutral):
        out = values
        for c in range(clips):
            keep = clip_rows((group, tok_dev), c, per_expert, group)
            out = jnp.where(keep, reduce(jnp.where(keep, values, neutral), axis=0, keepdims=True), out)
        return out

    peak = over_slots(peak, jnp.max, -jnp.inf)
    powers = jnp.exp(blocks - peak[None])
    norm = over_slots(jnp.sum(powers, axis=0), jnp.sum, 0.0)
    combine_ref[...] = (powers / norm[None]).reshape(rows, tok_dev).T.astype(BF16)

    acc[...] = jnp.zeros_like(acc)
    up_copy.wait()

    def expand(f, value):
        value = value.reshape(n_dp * group, width).astype(BF16)
        row0 = pl.multiple_of(f * width, width)
        acc[...] += jnp.dot(value, up[pl.ds(row0, width), :], preferred_element_type=F32)

    @pl.loop(staged, chunks)
    def _(f):
        await_bytes(rows_in.at[f, pl.ds(0, n_far)], direct_sem.at[1 + f - staged])
        value = rows_in[f, pl.ds(0, n_dp)].astype(F32)
        for k in range(1, n_y):
            value = value + rows_in[f, pl.ds(k * n_dp, n_dp)].astype(F32)
        expand(f, value)

    @pl.loop(0, staged)
    def _(f):
        await_bytes(rows_in.at[f, pl.ds(0, side + len(near))], slab_sem.at[1 + f])
        value = rows_in[f, pl.ds(near0, side)].astype(F32)
        for k in range(1, n_y):
            value = value + rows_in[f, pl.ds(k * n_dp + near0, side)].astype(F32)
        rows_in[f, pl.ds(near0, side)] = value.astype(BF16)
        expand(f, rows_in[f, pl.ds(0, n_dp)].astype(F32))

    value = acc[...]
    hidden[...] = (0.5 * value * (1.0 + lax.erf(value * np.float32(np.sqrt(0.5))))).astype(BF16)
    down_copy.wait()

    def contract(f):
        value = jnp.dot(hidden[...], down[:, lanes(f)], preferred_element_type=F32)
        result[f] = value.reshape(n_dp, group, width).astype(BF16)
        pool[f, core, y * n_dp + dp] = result[f, dp]

    @pl.loop(0, backed)
    def _(f):
        contract(f)
        for kd in range(side):
            back_copy(f, kd).start()

    for i in range(len(near)):
        back_near(i).start()

    @pl.loop(backed, chunks)
    def _(f):
        contract(f)

    for i in range(len(far)):
        back_direct(i).start()

    @pl.loop(0, backed)
    def _(f):
        await_bytes(result.at[f, pl.ds(0, side)], back_sem.at[1 + f])
        for ky in range(1, n_y):
            ysend_copy(f, ky).start()

    await_bytes(pool.at[pl.ds(0, backed), core, pl.ds(0, len(near))], back_near_sem.at[1])

    @pl.loop(0, backed)
    def _(f):
        await_bytes(from_y.at[f], ysend_sem.at[1 + f])
        forward_copy(f).start()

    await_bytes(pool.at[rest, core, pl.ds(0, n_far)], back_direct_sem.at[1])

    @pl.loop(backed, chunks)
    def _(f):
        forward_copy(f).start()

    @pl.loop(0, chunks)
    def _(f):
        forward_copy(f).wait_recv()
        gathered_ref[f] = pool[f].astype(F32).reshape(rows, width).astype(BF16)

    await_bytes(stats_in, stat_sem.at[0])
    await_bytes(from_core, core_sem.at[0])
    await_bytes(pool.at[:, core], fwd_sem.at[0])
    if staged:
        await_bytes(from_y.at[pl.ds(0, staged)], y_sem.at[0])
        await_bytes(chip.at[pl.ds(0, staged), pl.ds(0, side + len(near))], slab_sem.at[0])
    if staged < chunks:
        await_bytes(chip.at[pl.ds(0, chunks - staged), pl.ds(0, n_far)], direct_sem.at[0])
    if backed:
        await_bytes(from_y.at[pl.ds(0, backed)], ysend_sem.at[0])
        await_bytes(result.at[pl.ds(0, backed), pl.ds(0, side)], back_sem.at[0])
        await_bytes(chip.at[pl.ds(0, backed), pl.ds(0, len(near))], back_near_sem.at[0])
    if backed < chunks:
        await_bytes(chip.at[pl.ds(0, chunks - backed), pl.ds(0, n_far)], back_direct_sem.at[0])


def mix(clips, per_expert, chunks, width, parts, combine_ref, gathered_ref, out_hbm, stage, sem):
    tok_dev = combine_ref.shape[0]
    group = clips * per_expert
    size = tok_dev // parts
    copies = []
    for c in range(clips):
        for p in range(parts):
            piece = combine_ref[pl.ds(p * size, size), :]
            keep = clip_rows(piece.shape, c, per_expert, group, 1)
            weights = jnp.where(keep, piece.astype(F32), 0.0).astype(BF16)
            here = pl.ds(p * size, size)
            for f in range(chunks):
                stage[c, here, pl.ds(f * width, width)] = jnp.dot(
                    weights, gathered_ref[f], preferred_element_type=F32
                ).astype(BF16)
            copy = pltpu.make_async_copy(stage.at[c, here], out_hbm.at[c, here], sem.at[c, p])
            copy.start()
            copies.append(copy)
    for copy in copies:
        copy.wait()


def shards(n_dp, n_ctx, tokens, router, expert_up, expert_down):
    clips, tok_dev, feature = tokens.shape
    slots = router.shape[1]
    hidden = expert_up.shape[2]
    per_expert = slots // (n_dp * n_ctx)
    n_y = n_ctx // CORES
    group = clips * per_expert
    rows = n_dp * n_ctx * group
    width = 256
    parts = 4
    chunks = feature // width
    order = np.arange(slots).reshape(n_dp, n_y, CORES, 1, per_expert).transpose(2, 1, 0, 3, 4)
    order = np.broadcast_to(order, (CORES, n_y, n_dp, clips, per_expert)).reshape(-1)
    spread = jnp.asarray(order[:, None] == np.arange(slots)[None, :], BF16)
    staged, backed = 3, 2
    dims = (n_dp, n_ctx, clips, tok_dev, per_expert, chunks, width, staged, backed)
    vmem = pl.BlockSpec(memory_space=pltpu.VMEM)
    hbm = pl.BlockSpec(memory_space=pl.ANY)
    piece = (n_dp, group, width)
    dma = pltpu.SemaphoreType.DMA
    gathered, combine = pl.pallas_call(
        functools.partial(exchange, dims),
        out_shape=(
            pltpu.VMEM((chunks, rows, width), BF16),
            pltpu.VMEM((tok_dev, rows), BF16),
        ),
        in_specs=[hbm] * 5,
        out_specs=(vmem, vmem),
        scratch_shapes=[
            pltpu.VMEM((clips * tok_dev, feature), BF16),
            pltpu.VMEM((slots, feature), BF16),
            pltpu.VMEM((rows, slots), BF16),
            pltpu.VMEM((feature, rows), BF16),
            pltpu.VMEM((feature, hidden), BF16),
            pltpu.VMEM((hidden, feature), BF16),
            pltpu.VMEM((tok_dev, rows), F32),
            pltpu.VMEM((rows, tok_dev), F32),
            pltpu.VMEM((rows, clips * tok_dev), BF16),
            pltpu.VMEM((n_dp * group, hidden), F32),
            pltpu.VMEM((n_dp * group, hidden), BF16),
            pltpu.VMEM((chunks, CORES, n_y * n_dp, group, width), BF16),
            pltpu.VMEM((chunks, n_y * n_dp, group, width), BF16),
            pltpu.VMEM((chunks, n_y * n_dp, group, width), BF16),
            pltpu.VMEM((chunks, n_y - 1, n_dp // 2, group, width), BF16),
            pltpu.VMEM((chunks, n_dp // 2, group, width), BF16),
            pltpu.VMEM((chunks, n_y * n_dp, group, width), BF16),
            pltpu.VMEM((chunks,) + piece, BF16),
            pltpu.VMEM((chunks, CORES, n_y * n_dp, group, width), BF16),
            pltpu.VMEM((8, rows), F32),
            pltpu.VMEM((n_ctx - 1, 8, rows), F32),
            pltpu.VMEM((CORES, n_y * n_dp, group, 128), F32),
            dma((clips,)),
            dma((4,)),
            dma((2,)),
            dma((1 + chunks,)),
            dma((1 + staged,)),
            dma((1 + staged,)),
            dma((1 + chunks - staged,)),
            dma((1 + backed,)),
            dma((2,)),
            dma((2,)),
            dma((1 + backed,)),
            dma((1 + chunks,)),
        ],
        compiler_params=pltpu.CompilerParams(collective_id=0, has_side_effects=True, vmem_limit_bytes=58 * MIB),
        name="exchange",
    )(tokens, router.T, spread, expert_up, expert_down)
    gathered = pltpu.with_memory_space_constraint(gathered, pltpu.VMEM)
    combine = pltpu.with_memory_space_constraint(combine, pltpu.VMEM)
    return pl.pallas_call(
        functools.partial(mix, clips, per_expert, chunks, width, parts),
        out_shape=jax.ShapeDtypeStruct(tokens.shape, BF16),
        in_specs=[vmem, vmem],
        out_specs=hbm,
        scratch_shapes=[pltpu.VMEM(tokens.shape, BF16), dma((clips, parts))],
        compiler_params=pltpu.CompilerParams(vmem_limit_bytes=32 * MIB),
        name="mix",
    )(combine, gathered)


def solution(mesh):
    in_specs = (
        P("dp", "ctx", None),
        P(),
        P(("dp", "ctx"), None, None),
        P(("dp", "ctx"), None, None),
    )
    out_specs = P("dp", "ctx", None)
    body = functools.partial(shards, mesh.shape["dp"], mesh.shape["ctx"])
    return jax.shard_map(body, mesh=mesh, in_specs=in_specs, out_specs=out_specs, check_vma=False)
```
